256 devices in a mesh: grp: 2 (over core), row: 4 (over y), col: 32 (over z, x).
Axes of the slice: x: 4, y: 4, z: 8, core: 2. Of those that a mesh axis runs over, the one named last changes fastest.
Arguments:
- sub_rhs: float32 [2, 3, 4, 32, 256, 512], P('grp', None, 'row', 'col'), may hold values from -6 to 6
- sub_dinv: float32 [2, 3, 4, 32, 256, 256], P('grp', None, 'row', 'col')
- anc_rhs: float32 [4, 32, 256, 512], P('row', 'col'), may hold values from -6 to 6
- anc_dinv: float32 [4, 32, 256, 256], P('row', 'col')
- tiles: bfloat16 [2, 4, 32, 3, 16, 256, 256], P('grp', 'row', 'col'), may hold values from -0.09375 to 0.09375
- tile_target: int32 [2, 4, 32, 3, 16], P('grp', 'row', 'col'), may hold values from 0 to 11, as said below
- tile_source: int32 [2, 4, 32, 3, 16], P('grp', 'row', 'col'), may hold values from 0 to 31, as said below
- tile_count: int32 [2, 4, 32, 3], P('grp', 'row', 'col'), may hold values from 1 to 16, as said below
Outputs:
- sub_solution: float32 [2, 3, 4, 32, 256, 512], P('grp', None, 'row', 'col')
- anc_solution: float32 [4, 32, 256, 512], P('row', 'col')
The draws below stay inside these ranges and needn't reach their ends.
Inputs may be any that keep to these rules, and one draw needn't show every extreme that they name: `tile_target`: entry [g, q, c, k, j] is (t - 1) * 4 + r for a target level t with k < t <= 3 (t = 3 is the ancestor level) and a process row r; entries at slots j >= tile_count are unused. `tile_source`: Non-decreasing along the last dimension. `tile_count`: for every source level some device holds exactly 16 live tiles.
All inputs are finite; a program needn't handle non-finite values.
Results may differ from the reference program's by a relative error of at most 0.0027.
Values may be sent and summed in bfloat16 or wider, within the bound.
No kernel may reach another device: no remote copies, remote signals or barrier semaphores. Data moves between devices by JAX's collectives and lax.ppermute only.
A program may use at most 128 MiB of HBM per device.

```python
import math
import jax
import jax.numpy as jnp
from jax import lax

S = 256
LEV = 3
TPS = 16
W = 512
N_GRP = 2
N_ROW = 4
N_COL = 32


def inverse_blocks(key, shape):
    noise = jax.random.normal(key, shape, jnp.float32)
    return jnp.eye(S, dtype=jnp.float32) + 0.5 * noise / math.sqrt(S)


def draw_sub_dinv(key, part):
    return inverse_blocks(jax.random.fold_in(key, 11), (N_GRP, LEV, N_ROW, N_COL, S, S))


def draw_anc_dinv(key, part):
    return inverse_blocks(jax.random.fold_in(key, 13), (N_ROW, N_COL, S, S))


def draw_tile_target(key, part):
    shape = (N_GRP, N_ROW, N_COL, LEV, TPS)
    first_key, second_key = jax.random.split(jax.random.fold_in(key, 17))
    level_ids = lax.broadcasted_iota(jnp.int32, shape, 3)
    steps_up = jax.random.randint(first_key, shape, 0, 1048576) % (LEV - level_ids)
    target_rows = jax.random.randint(second_key, shape, 0, N_ROW)
    return ((level_ids + steps_up) * N_ROW + target_rows).astype(jnp.int32)


def draw_tile_source(key, part):
    shape = (N_GRP, N_ROW, N_COL, LEV, TPS)
    picked = jax.random.randint(jax.random.fold_in(key, 19), shape, 0, N_COL)
    return jnp.sort(picked, axis=-1).astype(jnp.int32)


def draw_tile_count(key, part):
    places = N_GRP * N_ROW * N_COL
    first_key, second_key = jax.random.split(jax.random.fold_in(key, 23))
    shifts = jax.random.randint(first_key, (places, LEV), 0, 4)
    base = jnp.maximum(TPS // jnp.left_shift(jnp.ones_like(shifts), shifts), 1)
    chosen = jax.random.randint(second_key, (LEV,), 0, places)
    place_ids = lax.broadcasted_iota(jnp.int32, (places, LEV), 0)
    counts = jnp.where(place_ids == chosen[None, :], TPS, base)
    return counts.reshape(N_GRP, N_ROW, N_COL, LEV).astype(jnp.int32)


def steps_of(key, dims, pieces, least, largest):
    factor_of = 1.0
    for axis_at, blocks in pieces:
        heights = jax.random.uniform(jax.random.fold_in(jax.random.fold_in(key, 6), axis_at), (blocks,), jnp.float32, least / len(pieces), largest / len(pieces))
        factor_of = factor_of * jnp.repeat(jnp.exp(heights), dims[axis_at] // blocks).reshape((-1,) + (1,) * (len(dims) - 1 - axis_at))
    return factor_of


def normal_values(key, shape, deviation, bound, cuts=(), kind=jnp.bfloat16):
    array = deviation * jax.random.normal(key, shape, jnp.float32)
    if cuts:
        array = array * steps_of(key, shape, cuts, -0.22, 0.18)
    return jnp.clip(array, -bound, bound).astype(kind)


def setup_inputs(seed: int = 0) -> dict:
    splits = jax.random.split(jax.random.key(seed), 9)
    return {
        "sub_rhs": normal_values(splits[0], (N_GRP, LEV, N_ROW, N_COL, S, W), 1.0, 6.0, ((0, 2), (2, 4), (3, 32)), jnp.float32),
        "sub_dinv": draw_sub_dinv(jax.random.fold_in(splits[8], 71), 0),
        "anc_rhs": normal_values(splits[2], (N_ROW, N_COL, S, W), 1.0, 6.0, ((0, 4), (1, 32)), jnp.float32),
        "anc_dinv": draw_anc_dinv(jax.random.fold_in(splits[8], 71), 0),
        "tiles": normal_values(splits[4], (N_GRP, N_ROW, N_COL, LEV, TPS, S, S), (S * TPS) ** -0.5, 0.09375, ((0, 2), (1, 4), (2, 32))),
        "tile_target": draw_tile_target(jax.random.fold_in(splits[8], 71), 0),
        "tile_source": draw_tile_source(jax.random.fold_in(splits[8], 71), 0),
        "tile_count": draw_tile_count(jax.random.fold_in(splits[8], 71), 0),
    }


def reference(sub_rhs, sub_dinv, anc_rhs, anc_dinv, tiles, tile_target, tile_source, tile_count):
    highest = lax.Precision.HIGHEST
    slot_ids = jnp.arange(TPS, dtype=jnp.int32)
    column_ids = jnp.broadcast_to(jnp.arange(N_COL, dtype=jnp.int32)[:, None], (N_COL, TPS))
    ancestor_sum = jnp.zeros((N_ROW, N_COL, S, W), jnp.float32)
    groups_out = []
    for group in range(N_GRP):
        pending = jnp.zeros((LEV * N_ROW, N_COL, S, W), jnp.float32)
        solved = []
        for source_level in range(LEV):
            remainder = sub_rhs[group, source_level]
            if source_level > 0:
                remainder = remainder - pending[(source_level - 1) * N_ROW:source_level * N_ROW]
            current = jnp.einsum("rcij,rcjw->rciw", sub_dinv[group, source_level], remainder, precision=highest)
            solved.append(current)
            rounded = current.astype(jnp.bfloat16)
            for proc_row in range(N_ROW):
                sources = tile_source[group, proc_row, :, source_level]
                targets = tile_target[group, proc_row, :, source_level]
                live = slot_ids[None, :] < tile_count[group, proc_row, :, source_level][:, None]
                fetched = rounded[proc_row][sources].astype(jnp.float32)
                blocks = tiles[group, proc_row, :, source_level].astype(jnp.float32)
                products = jnp.einsum("ctij,ctjw->ctiw", blocks, fetched, precision=highest)
                products = jnp.where(live[:, :, None, None], products, jnp.zeros_like(products))
                pending = pending.at[targets, column_ids].add(products)
        ancestor_sum = ancestor_sum + pending[(LEV - 1) * N_ROW:]
        groups_out.append(jnp.stack(solved))
    ancestor = jnp.einsum("rcij,rcjw->rciw", anc_dinv, anc_rhs - ancestor_sum, precision=highest)
    return jnp.stack(groups_out), ancestor
```

```python
import functools

import jax
import jax.numpy as jnp
import numpy as np
from jax import lax
from jax.experimental import pallas as pl
from jax.experimental.pallas import tpu as pltpu
from jax.sharding import PartitionSpec as P

Z, X = 8, 4
CHUNKS = 2
SEND = jnp.float32
UNROLL = 4
EARLY = 6
VMEM_PRODUCTS = 16 * 1024 * 1024
PART = {0: (0, 0), 6: (0, 1), 2: (0, 2), 4: (0, 3), 1: (1, 0), 7: (1, 1), 3: (1, 2), 5: (1, 3)}
FIRST = {0: (0, 1), 3: (2, 6), 1: (3, 5), 2: (4, 7)}
BYZ = {0: 0, 7: 2, 1: 3, 6: 4, 2: 5, 5: 6, 3: 7}
BYX = {0: 0, 3: 1, 1: 2, 2: 3}


def places():
    table = np.zeros((2, 32), np.int32)
    for dx in range(X):
        for dz in range(Z):
            half, block = PART[dz]
            table[0, dx * Z + dz] = FIRST[dx][half] * 4 + block
            at = BYX[dx]
            if dz == 4:
                table[1, dx * Z + dz] = (8 + at // 2) * 4 + at % 2
            else:
                table[1, dx * Z + dz] = BYZ[dz] * 4 + at
    return table


def pairs(first, second):
    out = []
    for group, move in ((0, first), (1, second)):
        if move is None:
            continue
        for z in range(Z):
            for x in range(X):
                to = ((z + move[0]) % Z) * X + (x + move[1]) % X
                out.append((group * Z * X + z * X + x, group * Z * X + to))
    return out


def hop(array, first, second):
    return lax.ppermute(array, ("grp", "col"), pairs(first, second))


def spread(own, core):
    s1 = hop(own, (2, 0), (0, 1))
    s2 = hop(own, (-2, 0), (0, -1))
    s3 = hop(own, (4, 0), (0, 2))
    near = jnp.stack([own, s1, s2, s3])
    l1 = hop(near, (0, 1), (1, 0))
    l2 = hop(near, (0, -1), (-1, 0))
    far = hop(near, (-1, 0), None)
    l1, l2, far = lax.optimization_barrier((l1, l2, far))
    l3 = hop(l1, (0, 1), (1, 0))
    l4 = hop(jnp.where(core == 0, far, l2), (0, -1), (-1, 0))
    l3, l4 = lax.optimization_barrier((l3, l4))
    l5 = hop(jnp.where(core == 0, far, l3), (0, 1), (1, 0))
    l6 = hop(l4, (0, -1), (-1, 0))
    l7 = hop(l3[:2], None, (2, 0))
    l8 = hop(l4[2:], None, (-2, 0))
    return [near, far, l1, l2, l3, l4, l5, l6, l7, l8]


def pick(index, low, high, action):
    if high - low == 1:
        action(low)
        return
    middle = (low + high) // 2

    @pl.when(index < middle)
    def _():
        pick(index, low, middle, action)

    @pl.when(index >= middle)
    def _():
        pick(index, middle, high, action)


def product_kernel(level, first, held, dump, last, has_carry, meta, tiles, *refs):
    arrays, refs = refs[:held], refs[held:]
    if has_carry:
        carry, refs = refs[0], refs[1:]
    if last:
        outs, (total, chosen, *rest) = refs[:-7], refs[-7:]
    else:
        total, (chosen, *rest) = refs[0], refs[1:]
    number, factor, block, factor_sem, block_sem = rest
    load = pltpu.make_async_copy(tiles.at[0, 0, 0, level], factor, factor_sem)
    load.start()
    number[0] = 0

    def fetch(j, nothing):
        place = meta[level, 16 + j]
        index = lax.div(place, 4)

        @pl.when((index >= first) & (index < first + held))
        def _():
            n = number[0]
            chosen[n] = j
            number[0] = n + 1

            def begin(i):
                pltpu.make_async_copy(
                    arrays[i].at[lax.rem(place, 4)], block.at[n], block_sem.at[n]
                ).start()

            pick(index - first, 0, held, begin)

        return nothing

    lax.fori_loop(0, meta[level, 32], fetch, 0)
    for slot in range(dump):
        if has_carry and slot < carry.shape[0]:
            total[slot] = carry[slot]
        else:
            total[slot] = jnp.zeros(total.shape[1:], jnp.float32)
    count = number[0]
    load.wait()

    def step(group, nothing):
        for k in range(UNROLL):
            n = group * UNROLL + k

            @pl.when(n < count)
            def _(n=n):
                pltpu.make_async_copy(arrays[0].at[0], block.at[n], block_sem.at[n]).wait()

        terms, targets = [], []
        for k in range(UNROLL):
            n = group * UNROLL + k
            live = n < count
            j = jnp.where(live, chosen[n], 0)
            targets.append(jnp.where(live, meta[level, j], dump))
            terms.append(jnp.dot(factor[j], block[n], preferred_element_type=jnp.float32))
        for target, term in zip(targets, terms):
            total[target] += term
        return nothing

    lax.fori_loop(0, lax.div(count + (UNROLL - 1), UNROLL), step, 0)
    if last:
        outs[0][...] = total[0]
        for slot in range(3):
            outs[1 + slot][...] = total[1 + slot].astype(SEND)
        for slot in range(dump - 4):
            outs[4][slot] = total[4 + slot]


def product_call(level, depth, meta, tiles, first, held, carry, last, name):
    rows, columns = held[0].shape[-2:]
    slots = tiles.shape[4]
    dump = 4 * (depth - level)
    vmem = pl.BlockSpec(memory_space=pltpu.VMEM)
    whole = jax.ShapeDtypeStruct((dump + 1, rows, columns), jnp.float32)
    if last:
        sent = jax.ShapeDtypeStruct((rows, columns), SEND)
        outs = [jax.ShapeDtypeStruct((rows, columns), jnp.float32), sent, sent, sent]
        if dump > 4:
            outs.append(jax.ShapeDtypeStruct((dump - 4, rows, columns), jnp.float32))
        scratch = [pltpu.VMEM(whole.shape, whole.dtype)]
    else:
        outs, scratch = [whole], []
    has_carry = carry is not None
    return pl.pallas_call(
        functools.partial(product_kernel, level, first, len(held), dump, last, has_carry),
        out_shape=outs,
        in_specs=[pl.BlockSpec(memory_space=pltpu.SMEM), pl.BlockSpec(memory_space=pltpu.HBM)]
        + [pl.BlockSpec(memory_space=pl.ANY)] * len(held)
        + [vmem] * has_carry,
        out_specs=[vmem] * len(outs),
        scratch_shapes=scratch
        + [
            pltpu.SMEM((slots,), jnp.int32),
            pltpu.SMEM((1,), jnp.int32),
            pltpu.VMEM((slots, rows, rows), jnp.bfloat16),
            pltpu.VMEM((slots, rows, columns), jnp.bfloat16),
            pltpu.SemaphoreType.DMA(()),
            pltpu.SemaphoreType.DMA((slots,)),
        ],
        compiler_params=pltpu.CompilerParams(vmem_limit_bytes=VMEM_PRODUCTS),
        cost_estimate=pl.CostEstimate(
            flops=slots * rows * rows * columns, bytes_accessed=4 * 1024 * 1024, transcendentals=0
        ),
        name=name,
    )(meta, tiles, *held, *([carry] if has_carry else []))


def products(level, depth, meta, tiles, held, carry):
    if EARLY:
        (carry,) = product_call(
            level, depth, meta, tiles, 0, held[:EARLY], carry, False, f"early_{level}"
        )
    return product_call(
        level, depth, meta, tiles, EARLY, held[EARLY:], carry, True, f"products_{level}"
    )


def solve_kernel(terms, narrow, inverse, rhs, *refs):
    rest = rhs[...]
    if terms:
        amount = refs[0][...].astype(jnp.float32)
        for term in refs[1:terms]:
            amount = amount + term[...].astype(jnp.float32)
        rest = rest - amount
    solved = jnp.dot(
        inverse[...], rest, precision=lax.Precision.HIGHEST, preferred_element_type=jnp.float32
    )
    refs[terms][...] = solved
    if narrow:
        refs[terms + 1][...] = solved.astype(jnp.bfloat16)


def solve(inverse, rhs, terms, narrow, name):
    vmem = pl.BlockSpec(memory_space=pltpu.VMEM)
    outs = [jax.ShapeDtypeStruct(rhs.shape, jnp.float32)]
    if narrow:
        outs.append(jax.ShapeDtypeStruct(rhs.shape, jnp.bfloat16))
    return pl.pallas_call(
        functools.partial(solve_kernel, len(terms), narrow),
        out_shape=outs,
        in_specs=[vmem] * (2 + len(terms)),
        out_specs=[vmem] * len(outs),
        compiler_params=pltpu.CompilerParams(vmem_limit_bytes=6 * 1024 * 1024),
        cost_estimate=pl.CostEstimate(
            flops=12 * rhs.shape[0] ** 2 * rhs.shape[1], bytes_accessed=2 * 1024 * 1024, transcendentals=0
        ),
        name=name,
    )(inverse, rhs, *terms)


def to_rows(sends):
    rows = 4
    return [
        lax.ppermute(part, "row", [(i, (i + away) % rows) for i in range(rows)])
        for away, part in zip((1, 2, 3), sends)
    ]


def tables(tile_target, tile_source, tile_count):
    core, row, col = lax.axis_index("grp"), lax.axis_index("row"), lax.axis_index("col")
    levels = jnp.arange(tile_target.shape[0], dtype=jnp.int32)[:, None]
    level_of, row_of = tile_target // 4, tile_target % 4
    target = (level_of - levels) * 4 + (row_of - row) % 4
    dz = (tile_source // X - col // X) % Z
    dx = (tile_source % X - col % X) % X
    key = dx * Z + dz
    known = jnp.asarray(places())
    known = jnp.where(core == 0, known[0], known[1])
    match = key[:, :, None] == jnp.arange(Z * X, dtype=jnp.int32)
    place = jnp.sum(jnp.where(match, known, 0), axis=-1)
    live = jnp.arange(tile_target.shape[1], dtype=jnp.int32)[None] < tile_count[:, None]
    target = jnp.where(live, target, 0)
    counts = jnp.broadcast_to(tile_count[:, None], target.shape)
    return jnp.concatenate([target, place, counts], axis=1).astype(jnp.int32)


def on_device(sub_rhs, sub_dinv, anc_rhs, anc_dinv, tiles, tile_target, tile_source, tile_count):
    rhs_levels = sub_rhs[0, :, 0, 0]
    inverses = sub_dinv[0, :, 0, 0]
    depth, block_rows, columns = rhs_levels.shape
    width = columns // CHUNKS
    core = lax.axis_index("grp")
    meta = tables(tile_target[0, 0, 0], tile_source[0, 0, 0], tile_count[0, 0, 0])
    cuts = [slice(i * width, (i + 1) * width) for i in range(CHUNKS)]
    terms = [()] * CHUNKS
    carry = [None] * CHUNKS
    solved = [[] for _ in range(CHUNKS)]
    for level in range(depth):
        for i in range(CHUNKS):
            wide, narrow = solve(
                inverses[level], rhs_levels[level][:, cuts[i]], terms[i], True, f"solve_{level}"
            )
            solved[i].append(wide)
            held = spread(narrow, core)
            mine, *sends = products(level, depth, meta, tiles, held, carry[i])
            if level + 1 < depth:
                carry[i] = sends.pop()
            terms[i] = (mine, *to_rows(sends))
    last = []
    for i in range(CHUNKS):
        part = sum(term.astype(jnp.float32) for term in terms[i])
        other = lax.ppermute(part, "grp", [(0, 1), (1, 0)])
        last.append(solve(anc_dinv[0, 0], anc_rhs[0, 0][:, cuts[i]], (part, other), False, "solve_top")[0])
    sub_out = jnp.concatenate([jnp.stack(chunk) for chunk in solved], axis=-1)
    top = jnp.concatenate(last, axis=-1)
    return sub_out[None, :, None, None], top[None, None]


def solution(mesh):
    placed = (
        P("grp", None, "row", "col", None, None),
        P("grp", None, "row", "col", None, None),
        P("row", "col", None, None),
        P("row", "col", None, None),
        P("grp", "row", "col", None, None, None, None),
        P("grp", "row", "col", None, None),
        P("grp", "row", "col", None, None),
        P("grp", "row", "col", None),
    )
    return jax.shard_map(
        on_device,
        mesh=mesh,
        in_specs=placed,
        out_specs=(P("grp", None, "row", "col", None, None), P("row", "col", None, None)),
        check_vma=False,
    )
```

```python
import functools

import jax
import jax.numpy as jnp
import numpy as np
from jax import lax
from jax.experimental import pallas as pl
from jax.experimental.pallas import tpu as pltpu
from jax.sharding import PartitionSpec as P

Z, X = 8, 4
UNROLL = 4
EARLY = 6
VMEM_PRODUCTS = 15 * 1024 * 1024
PART = {0: (0, 0), 6: (0, 1), 2: (0, 2), 4: (0, 3), 1: (1, 0), 3: (1, 1), 7: (1, 2), 5: (1, 3)}
FIRST = {0: (0, 1), 3: (2, 6), 1: (3, 5), 2: (4, 7)}
BYZ = {0: 0, 7: 2, 1: 3, 6: 4, 2: 5, 5: 6, 3: 7}
BYX = {0: 0, 3: 1, 1: 2, 2: 3}


def places():
    table = np.zeros((2, 32), np.int32)
    for dx in range(X):
        for dz in range(Z):
            half, block = PART[dz]
            table[0, dx * Z + dz] = FIRST[dx][half] * 4 + block
            at = BYX[dx]
            if dz == 4:
                table[1, dx * Z + dz] = (8 + at // 2) * 4 + at % 2
            else:
                table[1, dx * Z + dz] = BYZ[dz] * 4 + at
    return table


def pairs(first, second):
    out = []
    for group, move in ((0, first), (1, second)):
        if move is None:
            continue
        for z in range(Z):
            for x in range(X):
                to = ((z + move[0]) % Z) * X + (x + move[1]) % X
                out.append((group * Z * X + z * X + x, group * Z * X + to))
    return out


def hop(array, first, second):
    return lax.ppermute(array, ("grp", "col"), pairs(first, second))


def spread(own, core):
    s3 = hop(own, (4, 0), (0, 2))
    s1 = hop(own, (2, 0), (0, 1))
    s2 = hop(own, (-2, 0), (0, -1))
    near = jnp.stack([own, s1, s2, s3])
    l1 = hop(near, (0, 1), (1, 0))
    l2 = hop(near, (0, -1), (-1, 0))
    f1 = hop(near[0::2], (-1, 0), None)
    f2 = hop(near[0:2], (1, 0), None)
    l1, l2, f1, f2 = lax.optimization_barrier((l1, l2, f1, f2))
    far = jnp.concatenate([f1, f2])
    l3 = hop(l1, (0, 1), (1, 0))
    l4 = hop(jnp.where(core == 0, far, l2), (0, -1), (-1, 0))
    l3, l4 = lax.optimization_barrier((l3, l4))
    l5 = hop(jnp.where(core == 0, far, l3), (0, 1), (1, 0))
    l6 = hop(l4, (0, -1), (-1, 0))
    l7 = hop(l3[:2], None, (2, 0))
    l8 = hop(l4[2:], None, (-2, 0))
    return [near, far, l1, l2, l3, l4, l5, l6, l7, l8]


def pick(index, low, high, action):
    if high - low == 1:
        action(low)
        return
    middle = (low + high) // 2

    @pl.when(index < middle)
    def _():
        pick(index, low, middle, action)

    @pl.when(index >= middle)
    def _():
        pick(index, middle, high, action)


def product_kernel(level, first, held, dump, last, has_carry, meta, tiles, *refs):
    arrays, refs = refs[:held], refs[held:]
    if has_carry:
        carry, refs = refs[0], refs[1:]
    if last:
        outs, (total, chosen, *rest) = refs[:-7], refs[-7:]
    else:
        total, (chosen, *rest) = refs[0], refs[1:]
    number, factor, block, factor_sem, block_sem = rest
    load = pltpu.make_async_copy(tiles.at[0, 0, 0, level], factor, factor_sem)
    load.start()
    number[0] = 0

    def fetch(j, nothing):
        place = meta[level, 16 + j]
        index = lax.div(place, 4)

        @pl.when((index >= first) & (index < first + held))
        def _():
            n = number[0]
            chosen[n] = j
            number[0] = n + 1

            def begin(i):
                pltpu.make_async_copy(
                    arrays[i].at[lax.rem(place, 4)], block.at[n], block_sem.at[n]
                ).start()

            pick(index - first, 0, held, begin)

        return nothing

    lax.fori_loop(0, meta[level, 32], fetch, 0)
    for slot in range(dump):
        if has_carry and slot < carry.shape[0]:
            total[slot] = carry[slot]
        else:
            total[slot] = jnp.zeros(total.shape[1:], jnp.float32)
    count = number[0]
    load.wait()

    def step(group, nothing):
        for k in range(UNROLL):
            n = group * UNROLL + k

            @pl.when(n < count)
            def _(n=n):
                pltpu.make_async_copy(arrays[0].at[0], block.at[n], block_sem.at[n]).wait()

        terms, targets = [], []
        for k in range(UNROLL):
            n = group * UNROLL + k
            live = n < count
            j = jnp.where(live, chosen[n], 0)
            targets.append(jnp.where(live, meta[level, j], dump))
            terms.append(jnp.dot(factor[j], block[n], preferred_element_type=jnp.float32))
        for target, term in zip(targets, terms):
            total[target] += term
        return nothing

    lax.fori_loop(0, lax.div(count + (UNROLL - 1), UNROLL), step, 0)
    if last:
        outs[0][...] = total[0]
        for slot in range(3):
            outs[1 + slot][...] = total[1 + slot].astype(outs[1 + slot].dtype)
        for slot in range(dump - 4):
            outs[4][slot] = total[4 + slot]


def in_hbm(array):
    return pltpu.with_memory_space_constraint(array, pltpu.HBM)


def product_call(level, depth, meta, tiles, first, held, carry, last, name):
    rows, columns = held[0].shape[-2:]
    slots = tiles.shape[4]
    dump = 4 * (depth - level)
    vmem = pl.BlockSpec(memory_space=pltpu.VMEM)
    whole = jax.ShapeDtypeStruct((dump + 1, rows, columns), jnp.float32)
    if last:
        sent = jax.ShapeDtypeStruct((rows, columns), jnp.float32 if dump > 4 else jnp.bfloat16)
        outs = [jax.ShapeDtypeStruct((rows, columns), jnp.float32), sent, sent, sent]
        if dump > 4:
            outs.append(jax.ShapeDtypeStruct((dump - 4, rows, columns), jnp.float32))
        scratch = [pltpu.VMEM(whole.shape, whole.dtype)]
    else:
        outs, scratch = [whole], []
    has_carry = carry is not None
    return pl.pallas_call(
        functools.partial(product_kernel, level, first, len(held), dump, last, has_carry),
        out_shape=outs,
        in_specs=[pl.BlockSpec(memory_space=pltpu.SMEM), pl.BlockSpec(memory_space=pltpu.HBM)]
        + [pl.BlockSpec(memory_space=pl.ANY)] * len(held)
        + [vmem] * has_carry,
        out_specs=[vmem] * len(outs),
        scratch_shapes=scratch
        + [
            pltpu.SMEM((slots,), jnp.int32),
            pltpu.SMEM((1,), jnp.int32),
            pltpu.VMEM((slots, rows, rows), jnp.bfloat16),
            pltpu.VMEM((slots, rows, columns), jnp.bfloat16),
            pltpu.SemaphoreType.DMA(()),
            pltpu.SemaphoreType.DMA((slots,)),
        ],
        compiler_params=pltpu.CompilerParams(vmem_limit_bytes=VMEM_PRODUCTS),
        cost_estimate=pl.CostEstimate(
            flops=slots * rows * rows * columns, bytes_accessed=4 * 1024 * 1024, transcendentals=0
        ),
        name=name,
    )(meta, in_hbm(tiles), *held, *([carry] if has_carry else []))


def products(level, depth, meta, tiles, held, carry):
    if EARLY:
        (carry,) = product_call(
            level, depth, meta, tiles, 0, held[:EARLY], carry, False, f"early_{level}"
        )
    return product_call(
        level, depth, meta, tiles, EARLY, held[EARLY:], carry, True, f"products_{level}"
    )


def solve_kernel(terms, narrow, inverse, rhs, *refs):
    rest = rhs[...].reshape(rhs.shape[-2:])
    if terms:
        amount = refs[0][...].astype(jnp.float32)
        for term in refs[1:terms]:
            amount = amount + term[...].astype(jnp.float32)
        rest = rest - amount
    solved = jnp.dot(
        inverse[...].reshape(inverse.shape[-2:]),
        rest,
        precision=lax.Precision.HIGHEST,
        preferred_element_type=jnp.float32,
    )
    refs[terms][...] = solved
    if narrow:
        refs[terms + 1][...] = solved.astype(jnp.bfloat16)


def solve(level, inverse, rhs, terms, narrow, name):
    rows, columns = rhs.shape[-2:]
    vmem = pl.BlockSpec(memory_space=pltpu.VMEM)
    outs = [jax.ShapeDtypeStruct((rows, columns), jnp.float32)]
    if narrow:
        outs.append(jax.ShapeDtypeStruct((rows, columns), jnp.bfloat16))

    if level is None or level == 0:
        operands = (in_hbm(inverse), in_hbm(rhs))
    else:
        operands = (inverse[0, level, 0, 0], rhs[0, level, 0, 0])

    def of_level(array):
        if array.ndim == 2:
            return vmem
        block = (1,) * (array.ndim - 2) + array.shape[-2:]
        at = (0,) * array.ndim if level is None else (0, level) + (0,) * (array.ndim - 2)
        return pl.BlockSpec(block, lambda i: at)

    return pl.pallas_call(
        functools.partial(solve_kernel, len(terms), narrow),
        out_shape=outs,
        grid=(1,),
        in_specs=[of_level(array) for array in operands] + [vmem] * len(terms),
        out_specs=[vmem] * len(outs),
        compiler_params=pltpu.CompilerParams(vmem_limit_bytes=6 * 1024 * 1024),
        cost_estimate=pl.CostEstimate(
            flops=12 * rows * rows * columns, bytes_accessed=2 * 1024 * 1024, transcendentals=0
        ),
        name=name,
    )(*operands, *terms)


def to_rows(sends):
    rows = 4
    return [
        lax.ppermute(part, "row", [(i, (i + away) % rows) for i in range(rows)])
        for away, part in zip((1, 2, 3), sends)
    ]


def tables(tile_target, tile_source, tile_count):
    core, row, col = lax.axis_index("grp"), lax.axis_index("row"), lax.axis_index("col")
    levels = jnp.arange(tile_target.shape[0], dtype=jnp.int32)[:, None]
    level_of, row_of = tile_target // 4, tile_target % 4
    target = (level_of - levels) * 4 + (row_of - row) % 4
    dz = (tile_source // X - col // X) % Z
    dx = (tile_source % X - col % X) % X
    key = dx * Z + dz
    known = jnp.asarray(places())
    known = jnp.where(core == 0, known[0], known[1])
    match = key[:, :, None] == jnp.arange(Z * X, dtype=jnp.int32)
    place = jnp.sum(jnp.where(match, known, 0), axis=-1)
    live = jnp.arange(tile_target.shape[1], dtype=jnp.int32)[None] < tile_count[:, None]
    target = jnp.where(live, target, 0)
    counts = jnp.broadcast_to(tile_count[:, None], target.shape)
    return jnp.concatenate([target, place, counts], axis=1).astype(jnp.int32)


def on_device(sub_rhs, sub_dinv, anc_rhs, anc_dinv, tiles, tile_target, tile_source, tile_count):
    depth = sub_rhs.shape[1]
    core = lax.axis_index("grp")
    meta = tables(tile_target[0, 0, 0], tile_source[0, 0, 0], tile_count[0, 0, 0])
    terms, carry, solved = (), None, []
    for level in range(depth):
        wide, narrow = solve(level, sub_dinv, sub_rhs, terms, True, f"solve_{level}")
        solved.append(wide)
        held = spread(narrow, core)
        mine, *sends = products(level, depth, meta, tiles, held, carry)
        if level + 1 < depth:
            carry = sends.pop()
        terms = (mine, *to_rows(sends))
    part = sum(term.astype(jnp.float32) for term in terms)
    other = lax.ppermute(part, "grp", [(0, 1), (1, 0)])
    (top,) = solve(None, anc_dinv, anc_rhs, (part, other), False, "solve_top")
    return jnp.stack(solved)[None, :, None, None], top[None, None]


def solution(mesh):
    placed = (
        P("grp", None, "row", "col", None, None),
        P("grp", None, "row", "col", None, None),
        P("row", "col", None, None),
        P("row", "col", None, None),
        P("grp", "row", "col", None, None, None, None),
        P("grp", "row", "col", None, None),
        P("grp", "row", "col", None, None),
        P("grp", "row", "col", None),
    )
    return jax.shard_map(
        on_device,
        mesh=mesh,
        in_specs=placed,
        out_specs=(P("grp", None, "row", "col", None, None), P("row", "col", None, None)),
        check_vma=False,
    )
```

```python
import functools

import jax
import jax.numpy as jnp
import numpy as np
from jax import lax
from jax.experimental import pallas as pl
from jax.experimental.pallas import tpu as pltpu
from jax.sharding import PartitionSpec as P

Z, X = 8, 4
UNROLL = 4
EARLY = 6
PARTS = 2
VMEM_PRODUCTS = 8 * 1024 * 1024
PART = {0: (0, 0), 6: (0, 1), 2: (0, 2), 4: (0, 3), 1: (1, 0), 3: (1, 1), 7: (1, 2), 5: (1, 3)}
FIRST = {0: (0, 1), 3: (2, 6), 1: (3, 5), 2: (4, 7)}
BYZ = {0: 0, 7: 2, 1: 3, 6: 4, 2: 5, 5: 6, 3: 7}
BYX = {0: 0, 3: 1, 1: 2, 2: 3}


def places():
    table = np.zeros((2, 32), np.int32)
    for dx in range(X):
        for dz in range(Z):
            half, block = PART[dz]
            table[0, dx * Z + dz] = FIRST[dx][half] * 4 + block
            at = BYX[dx]
            if dz == 4:
                table[1, dx * Z + dz] = (8 + at // 2) * 4 + at % 2
            else:
                table[1, dx * Z + dz] = BYZ[dz] * 4 + at
    return table


def pairs(first, second):
    out = []
    for group, move in ((0, first), (1, second)):
        if move is None:
            continue
        for z in range(Z):
            for x in range(X):
                to = ((z + move[0]) % Z) * X + (x + move[1]) % X
                out.append((group * Z * X + z * X + x, group * Z * X + to))
    return out


def hop(array, first, second):
    return lax.ppermute(array, ("grp", "col"), pairs(first, second))


def spread(owns, core, tables_done):
    nears = []
    for own in owns:
        s3 = hop(own, (4, 0), (0, 2))
        s1 = hop(own, (2, 0), (0, 1))
        s2 = hop(own, (-2, 0), (0, -1))
        nears.append(jnp.stack([own, s1, s2, s3]))
    near = jnp.concatenate(nears, axis=-1)
    if tables_done is not None:
        near, _ = lax.optimization_barrier((near, tables_done))
    l1 = hop(near, (0, 1), (1, 0))
    l2 = hop(near, (0, -1), (-1, 0))
    f1 = hop(near[0::2], (-1, 0), None)
    f2 = hop(near[0:2], (1, 0), None)
    l1, l2, f1, f2 = lax.optimization_barrier((l1, l2, f1, f2))
    far = jnp.concatenate([f1, f2])
    l3 = hop(l1, (0, 1), (1, 0))
    l4 = hop(jnp.where(core == 0, far, l2), (0, -1), (-1, 0))
    l3, l4 = lax.optimization_barrier((l3, l4))
    l5 = hop(jnp.where(core == 0, far, l3), (0, 1), (1, 0))
    l6 = hop(l4, (0, -1), (-1, 0))
    l7 = hop(l3[:2], None, (2, 0))
    l8 = hop(l4[2:], None, (-2, 0))
    return [near, far, l1, l2, l3, l4, l5, l6, l7, l8]


def pick(index, low, high, action):
    if high - low == 1:
        action(low)
        return
    middle = (low + high) // 2

    @pl.when(index < middle)
    def _():
        pick(index, low, middle, action)

    @pl.when(index >= middle)
    def _():
        pick(index, middle, high, action)


def product_kernel(level, first, held, dump, last, has_carry, meta, tiles, *refs):
    arrays, refs = refs[:held], refs[held:]
    if has_carry:
        carry, refs = refs[0], refs[1:]
    outs, (total, chosen, *rest) = refs[:-7], refs[-7:]
    number, factor, block, factor_sem, block_sem = rest
    load = pltpu.make_async_copy(tiles.at[0, 0, 0, level], factor, factor_sem)
    load.start()
    number[0] = 0

    def fetch(j, nothing):
        place = meta[level, 16 + j]
        index = lax.div(place, 4)

        @pl.when((index >= first) & (index < first + held))
        def _():
            n = number[0]
            chosen[n] = j
            number[0] = n + 1

            def begin(i):
                pltpu.make_async_copy(
                    arrays[i].at[lax.rem(place, 4)], block.at[n], block_sem.at[n]
                ).start()

            pick(index - first, 0, held, begin)

        return nothing

    lax.fori_loop(0, meta[level, 32], fetch, 0)
    if not last:
        for slot in range(dump):
            if has_carry:
                total[slot] = carry[4 + slot]
            else:
                total[slot] = jnp.zeros(total.shape[1:], jnp.float32)
    count = number[0]
    load.wait()

    def step(group, nothing):
        for k in range(UNROLL):
            n = group * UNROLL + k

            @pl.when(n < count)
            def _(n=n):
                pltpu.make_async_copy(arrays[0].at[0], block.at[n], block_sem.at[n]).wait()

        terms, targets = [], []
        for k in range(UNROLL):
            n = group * UNROLL + k
            live = n < count
            j = jnp.where(live, chosen[n], 0)
            targets.append(jnp.where(live, meta[level, j], dump))
            terms.append(jnp.dot(factor[j], block[n], preferred_element_type=jnp.float32))
        for target, term in zip(targets, terms):
            total[target] += term
        return nothing

    lax.fori_loop(0, lax.div(count + (UNROLL - 1), UNROLL), step, 0)
    if last:
        width = outs[0].shape[1]
        for n, out in enumerate(outs):
            cut = pl.ds((n // 4) * width, width)
            out[...] = total[n % 4, :, cut].astype(out.dtype)


def in_hbm(array):
    return pltpu.with_memory_space_constraint(array, pltpu.HBM)


def product_call(level, depth, meta, tiles, first, held, carry, last, name):
    rows, columns = held[0].shape[-2:]
    slots = tiles.shape[4]
    dump = 4 * (depth - level)
    vmem = pl.BlockSpec(memory_space=pltpu.VMEM)
    whole = jax.ShapeDtypeStruct((dump + 1, rows, columns), jnp.float32)
    outs, aliases = [whole], {}
    if last:
        parts = PARTS if dump > 4 else 1
        shape = (rows, columns // parts)
        sent = jax.ShapeDtypeStruct(shape, jnp.float32 if dump > 4 else jnp.bfloat16)
        outs = [jax.ShapeDtypeStruct(shape, jnp.float32), sent, sent, sent] * parts + [whole]
        aliases = {2 + len(held): len(outs) - 1}
    has_carry = carry is not None
    return pl.pallas_call(
        functools.partial(product_kernel, level, first, len(held), dump, last, has_carry),
        out_shape=outs,
        in_specs=[pl.BlockSpec(memory_space=pltpu.SMEM), pl.BlockSpec(memory_space=pltpu.HBM)]
        + [pl.BlockSpec(memory_space=pl.ANY)] * len(held)
        + [vmem] * has_carry,
        out_specs=[vmem] * len(outs),
        input_output_aliases=aliases,
        scratch_shapes=[
            pltpu.SMEM((slots,), jnp.int32),
            pltpu.SMEM((1,), jnp.int32),
            pltpu.VMEM((slots, rows, rows), jnp.bfloat16),
            pltpu.VMEM((slots, rows, columns), jnp.bfloat16),
            pltpu.SemaphoreType.DMA(()),
            pltpu.SemaphoreType.DMA((slots,)),
        ],
        compiler_params=pltpu.CompilerParams(vmem_limit_bytes=VMEM_PRODUCTS),
        cost_estimate=pl.CostEstimate(
            flops=slots * rows * rows * columns, bytes_accessed=4 * 1024 * 1024, transcendentals=0
        ),
        name=name,
    )(meta, in_hbm(tiles), *held, *([carry] if has_carry else []))


def products(level, depth, meta, tiles, held, carry):
    if EARLY:
        (carry,) = product_call(
            level, depth, meta, tiles, 0, held[:EARLY], carry, False, f"early_{level}"
        )
    return product_call(
        level, depth, meta, tiles, EARLY, held[EARLY:], carry, True, f"products_{level}"
    )


def solve_kernel(terms, narrow, inverse, rhs, *refs):
    rest = rhs[...].reshape(rhs.shape[-2:])
    if terms:
        amount = refs[0][...].astype(jnp.float32)
        for term in refs[1:terms]:
            amount = amount + term[...].astype(jnp.float32)
        rest = rest - amount
    solved = jnp.dot(
        inverse[...].reshape(inverse.shape[-2:]),
        rest,
        precision=lax.Precision.HIGHEST,
        preferred_element_type=jnp.float32,
    )
    refs[terms][...] = solved
    if narrow:
        refs[terms + 1][...] = solved.astype(jnp.bfloat16)


def solve(level, inverse, rhs, part, terms, narrow, name):
    rows, columns = terms[0].shape if terms else rhs.shape[-2:]
    vmem = pl.BlockSpec(memory_space=pltpu.VMEM)
    outs = [jax.ShapeDtypeStruct((rows, columns), jnp.float32)]
    if narrow:
        outs.append(jax.ShapeDtypeStruct((rows, columns), jnp.bfloat16))

    if level is None or level == 0:
        operands = (in_hbm(inverse), in_hbm(rhs))
    else:
        cut = slice(part * columns, (part + 1) * columns)
        operands = (inverse[0, level, 0, 0], rhs[0, level, 0, 0][:, cut])

    def of_level(array):
        if array.ndim == 2:
            return vmem
        block = (1,) * (array.ndim - 2) + array.shape[-2:]
        at = (0,) * array.ndim if level is None else (0, level) + (0,) * (array.ndim - 2)
        return pl.BlockSpec(block, lambda i: at)

    return pl.pallas_call(
        functools.partial(solve_kernel, len(terms), narrow),
        out_shape=outs,
        grid=(1,),
        in_specs=[of_level(array) for array in operands] + [vmem] * len(terms),
        out_specs=[vmem] * len(outs),
        compiler_params=pltpu.CompilerParams(vmem_limit_bytes=6 * 1024 * 1024),
        cost_estimate=pl.CostEstimate(
            flops=12 * rows * rows * columns, bytes_accessed=2 * 1024 * 1024, transcendentals=0
        ),
        name=name,
    )(*operands, *terms)


def to_rows(sends):
    rows = 4
    return [
        lax.ppermute(part, "row", [(i, (i + away) % rows) for i in range(rows)])
        for away, part in zip((1, 2, 3), sends)
    ]


def tables(tile_target, tile_source, tile_count):
    core, row, col = lax.axis_index("grp"), lax.axis_index("row"), lax.axis_index("col")
    levels = jnp.arange(tile_target.shape[0], dtype=jnp.int32)[:, None]
    level_of, row_of = tile_target // 4, tile_target % 4
    target = (level_of - levels) * 4 + (row_of - row) % 4
    dz = (tile_source // X - col // X) % Z
    dx = (tile_source % X - col % X) % X
    key = dx * Z + dz
    known = jnp.asarray(places())
    known = jnp.where(core == 0, known[0], known[1])
    match = key[:, :, None] == jnp.arange(Z * X, dtype=jnp.int32)
    place = jnp.sum(jnp.where(match, known, 0), axis=-1)
    live = jnp.arange(tile_target.shape[1], dtype=jnp.int32)[None] < tile_count[:, None]
    target = jnp.where(live, target, 0)
    counts = jnp.broadcast_to(tile_count[:, None], target.shape)
    return jnp.concatenate([target, place, counts], axis=1).astype(jnp.int32)


def on_device(sub_rhs, sub_dinv, anc_rhs, anc_dinv, tiles, tile_target, tile_source, tile_count):
    depth = sub_rhs.shape[1]
    core = lax.axis_index("grp")
    meta = tables(tile_target[0, 0, 0], tile_source[0, 0, 0], tile_count[0, 0, 0])
    parts, carry, solved = [()], None, []
    for level in range(depth):
        both = [
            solve(level, sub_dinv, sub_rhs, i, terms, True, f"solve_{level}_{i}")
            for i, terms in enumerate(parts)
        ]
        solved.append(jnp.concatenate([wide for wide, _ in both], axis=-1))
        held = spread([narrow for _, narrow in both], core, None if level else meta)
        *sums, carry = products(level, depth, meta, tiles, held, carry)
        parts = [(sums[n], *to_rows(sums[n + 1 : n + 4])) for n in range(0, len(sums), 4)]
    part = sum(term.astype(jnp.float32) for term in parts[0])
    other = lax.ppermute(part, "grp", [(0, 1), (1, 0)])
    (top,) = solve(None, anc_dinv, anc_rhs, 0, (part, other), False, "solve_top")
    return jnp.stack(solved)[None, :, None, None], top[None, None]


def solution(mesh):
    placed = (
        P("grp", None, "row", "col", None, None),
        P("grp", None, "row", "col", None, None),
        P("row", "col", None, None),
        P("row", "col", None, None),
        P("grp", "row", "col", None, None, None, None),
        P("grp", "row", "col", None, None),
        P("grp", "row", "col", None, None),
        P("grp", "row", "col", None),
    )
    return jax.shard_map(
        on_device,
        mesh=mesh,
        in_specs=placed,
        out_specs=(P("grp", None, "row", "col", None, None), P("row", "col", None, None)),
        check_vma=False,
    )
```

```python
import functools

import jax
import jax.numpy as jnp
import numpy as np
from jax import lax
from jax.experimental import pallas as pl
from jax.experimental.pallas import tpu as pltpu
from jax.sharding import PartitionSpec as P

Z, X = 8, 4
UNROLL = 4
EARLY = 6
PARTS = 2
VMEM_PRODUCTS = 8 * 1024 * 1024
PART = {0: (0, 0), 4: (0, 1), 6: (0, 2), 2: (0, 3), 1: (1, 0), 5: (1, 1), 7: (1, 2), 3: (1, 3)}
FIRST = {0: (0, 1), 3: (2, 6), 1: (3, 5), 2: (4, 7)}
BYZ = {0: 0, 7: 2, 1: 3, 6: 4, 2: 5, 5: 6, 3: 7}
BYX = {0: 0, 2: 1, 3: 2, 1: 3}


def places():
    table = np.zeros((2, 32), np.int32)
    for dx in range(X):
        for dz in range(Z):
            half, block = PART[dz]
            table[0, dx * Z + dz] = FIRST[dx][half] * 4 + block
            at = BYX[dx]
            if dz == 4:
                table[1, dx * Z + dz] = (8 + at // 2) * 4 + at % 2
            else:
                table[1, dx * Z + dz] = BYZ[dz] * 4 + at
    return table


def pairs(first, second):
    out = []
    for group, move in ((0, first), (1, second)):
        if move is None:
            continue
        for z in range(Z):
            for x in range(X):
                to = ((z + move[0]) % Z) * X + (x + move[1]) % X
                out.append((group * Z * X + z * X + x, group * Z * X + to))
    return out


def hop(array, first, second):
    return lax.ppermute(array, ("grp", "col"), pairs(first, second))


def spread(owns, core, tables_done):
    nears = []
    for own in owns:
        s1 = hop(own, (2, 0), (0, 1))
        s2 = hop(own, (-2, 0), (0, -1))
        s3 = hop(own, (4, 0), (0, 2))
        nears.append(jnp.stack([own, s3, s1, s2]))
    near = jnp.concatenate(nears, axis=-1)
    if tables_done is not None:
        near, _ = lax.optimization_barrier((near, tables_done))
    l1 = hop(near, (0, 1), (1, 0))
    l2 = hop(near, (0, -1), (-1, 0))
    f1 = hop(near[:2], (-1, 0), None)
    f2 = hop(near[:2], (1, 0), None)
    l1, l2, f1, f2 = lax.optimization_barrier((l1, l2, f1, f2))
    far = jnp.concatenate([f1, f2])
    l3 = hop(l1, (0, 1), (1, 0))
    l4 = hop(jnp.where(core == 0, far, l2), (0, -1), (-1, 0))
    l3, l4 = lax.optimization_barrier((l3, l4))
    l5 = hop(jnp.where(core == 0, far, l3), (0, 1), (1, 0))
    l6 = hop(l4, (0, -1), (-1, 0))
    l7 = hop(l3[:2], None, (2, 0))
    l8 = hop(l4[2:], None, (-2, 0))
    return [near, far, l1, l2, l3, l4, l5, l6, l7, l8]


def pick(index, low, high, action):
    if high - low == 1:
        action(low)
        return
    middle = (low + high) // 2

    @pl.when(index < middle)
    def _():
        pick(index, low, middle, action)

    @pl.when(index >= middle)
    def _():
        pick(index, middle, high, action)


def product_kernel(level, first, held, dump, last, has_carry, meta, tiles, *refs):
    arrays, refs = refs[:held], refs[held:]
    if has_carry:
        carry, refs = refs[0], refs[1:]
    outs, (total, chosen, *rest) = refs[:-7], refs[-7:]
    number, factor, block, factor_sem, block_sem = rest
    load = pltpu.make_async_copy(tiles.at[0, 0, 0, level], factor, factor_sem)
    load.start()
    number[0] = 0

    def fetch(j, nothing):
        place = meta[level, 16 + j]
        index = lax.div(place, 4)

        @pl.when((index >= first) & (index < first + held))
        def _():
            n = number[0]
            chosen[n] = j
            number[0] = n + 1

            def begin(i):
                pltpu.make_async_copy(
                    arrays[i].at[lax.rem(place, 4)], block.at[n], block_sem.at[n]
                ).start()

            pick(index - first, 0, held, begin)

        return nothing

    lax.fori_loop(0, meta[level, 32], fetch, 0)
    if not last:
        for slot in range(dump):
            if has_carry:
                total[slot] = carry[4 + slot]
            else:
                total[slot] = jnp.zeros(total.shape[1:], jnp.float32)
    count = number[0]
    load.wait()

    def step(group, nothing):
        for k in range(UNROLL):
            n = group * UNROLL + k

            @pl.when(n < count)
            def _(n=n):
                pltpu.make_async_copy(arrays[0].at[0], block.at[n], block_sem.at[n]).wait()

        terms, targets = [], []
        for k in range(UNROLL):
            n = group * UNROLL + k
            live = n < count
            j = jnp.where(live, chosen[n], 0)
            targets.append(jnp.where(live, meta[level, j], dump))
            terms.append(jnp.dot(factor[j], block[n], preferred_element_type=jnp.float32))
        for target, term in zip(targets, terms):
            total[target] += term
        return nothing

    lax.fori_loop(0, lax.div(count + (UNROLL - 1), UNROLL), step, 0)
    if last:
        width = outs[0].shape[1]
        for n, out in enumerate(outs):
            cut = pl.ds((n // 4) * width, width)
            out[...] = total[n % 4, :, cut].astype(out.dtype)


def in_hbm(array):
    return pltpu.with_memory_space_constraint(array, pltpu.HBM)


def product_call(level, depth, meta, tiles, first, held, carry, last, name):
    rows, columns = held[0].shape[-2:]
    slots = tiles.shape[4]
    dump = 4 * (depth - level)
    vmem = pl.BlockSpec(memory_space=pltpu.VMEM)
    whole = jax.ShapeDtypeStruct((dump + 1, rows, columns), jnp.float32)
    outs, aliases = [whole], {}
    if last:
        parts = PARTS if dump > 4 else 1
        shape = (rows, columns // parts)
        sent = jax.ShapeDtypeStruct(shape, jnp.float32 if dump > 4 else jnp.bfloat16)
        outs = [jax.ShapeDtypeStruct(shape, jnp.float32), sent, sent, sent] * parts + [whole]
        aliases = {2 + len(held): len(outs) - 1}
    has_carry = carry is not None
    return pl.pallas_call(
        functools.partial(product_kernel, level, first, len(held), dump, last, has_carry),
        out_shape=outs,
        in_specs=[pl.BlockSpec(memory_space=pltpu.SMEM), pl.BlockSpec(memory_space=pltpu.HBM)]
        + [pl.BlockSpec(memory_space=pl.ANY)] * len(held)
        + [vmem] * has_carry,
        out_specs=[vmem] * len(outs),
        input_output_aliases=aliases,
        scratch_shapes=[
            pltpu.SMEM((slots,), jnp.int32),
            pltpu.SMEM((1,), jnp.int32),
            pltpu.VMEM((slots, rows, rows), jnp.bfloat16),
            pltpu.VMEM((slots, rows, columns), jnp.bfloat16),
            pltpu.SemaphoreType.DMA(()),
            pltpu.SemaphoreType.DMA((slots,)),
        ],
        compiler_params=pltpu.CompilerParams(vmem_limit_bytes=VMEM_PRODUCTS),
        cost_estimate=pl.CostEstimate(
            flops=slots * rows * rows * columns, bytes_accessed=4 * 1024 * 1024, transcendentals=0
        ),
        name=name,
    )(meta, in_hbm(tiles), *held, *([carry] if has_carry else []))


def products(level, depth, meta, tiles, held, carry):
    if EARLY:
        (carry,) = product_call(
            level, depth, meta, tiles, 0, held[:EARLY], carry, False, f"early_{level}"
        )
    return product_call(
        level, depth, meta, tiles, EARLY, held[EARLY:], carry, True, f"products_{level}"
    )


def solve_kernel(terms, narrow, inverse, rhs, *refs):
    rest = rhs[...].reshape(rhs.shape[-2:])
    if terms:
        amount = refs[0][...].astype(jnp.float32)
        for term in refs[1:terms]:
            amount = amount + term[...].astype(jnp.float32)
        rest = rest - amount
    solved = jnp.dot(
        inverse[...].reshape(inverse.shape[-2:]),
        rest,
        precision=lax.Precision.HIGHEST,
        preferred_element_type=jnp.float32,
    )
    refs[terms][...] = solved
    if narrow:
        refs[terms + 1][...] = solved.astype(jnp.bfloat16)


def solve(level, inverse, rhs, part, terms, narrow, name):
    rows, columns = terms[0].shape if terms else rhs.shape[-2:]
    vmem = pl.BlockSpec(memory_space=pltpu.VMEM)
    outs = [jax.ShapeDtypeStruct((rows, columns), jnp.float32)]
    if narrow:
        outs.append(jax.ShapeDtypeStruct((rows, columns), jnp.bfloat16))

    if level is None:
        operands = (inverse[0, 0], rhs[0, 0])
    elif level == 0:
        operands = (in_hbm(inverse), in_hbm(rhs))
    else:
        cut = slice(part * columns, (part + 1) * columns)
        operands = (inverse[0, level, 0, 0], rhs[0, level, 0, 0][:, cut])

    def of_level(array):
        if array.ndim == 2:
            return vmem
        block = (1,) * (array.ndim - 2) + array.shape[-2:]
        return pl.BlockSpec(block, lambda i: (0, level) + (0,) * (array.ndim - 2))

    return pl.pallas_call(
        functools.partial(solve_kernel, len(terms), narrow),
        out_shape=outs,
        grid=(1,),
        in_specs=[of_level(array) for array in operands] + [vmem] * len(terms),
        out_specs=[vmem] * len(outs),
        compiler_params=pltpu.CompilerParams(vmem_limit_bytes=6 * 1024 * 1024),
        cost_estimate=pl.CostEstimate(
            flops=12 * rows * rows * columns, bytes_accessed=2 * 1024 * 1024, transcendentals=0
        ),
        name=name,
    )(*operands, *terms)


def to_rows(sends):
    rows = 4
    return [
        lax.ppermute(sends[away - 1], "row", [(i, (i + away) % rows) for i in range(rows)])
        for away in (2, 1, 3)
    ]


def tables(tile_target, tile_source, tile_count):
    core, row, col = lax.axis_index("grp"), lax.axis_index("row"), lax.axis_index("col")
    levels = jnp.arange(tile_target.shape[0], dtype=jnp.int32)[:, None]
    level_of, row_of = tile_target // 4, tile_target % 4
    target = (level_of - levels) * 4 + (row_of - row) % 4
    dz = (tile_source // X - col // X) % Z
    dx = (tile_source % X - col % X) % X
    key = dx * Z + dz
    known = jnp.asarray(places())
    known = jnp.where(core == 0, known[0], known[1])
    match = key[:, :, None] == jnp.arange(Z * X, dtype=jnp.int32)
    place = jnp.sum(jnp.where(match, known, 0), axis=-1)
    live = jnp.arange(tile_target.shape[1], dtype=jnp.int32)[None] < tile_count[:, None]
    target = jnp.where(live, target, 0)
    counts = jnp.broadcast_to(tile_count[:, None], target.shape)
    return jnp.concatenate([target, place, counts], axis=1).astype(jnp.int32)


def on_device(sub_rhs, sub_dinv, anc_rhs, anc_dinv, tiles, tile_target, tile_source, tile_count):
    depth = sub_rhs.shape[1]
    core = lax.axis_index("grp")
    meta = tables(tile_target[0, 0, 0], tile_source[0, 0, 0], tile_count[0, 0, 0])
    parts, carry, solved = [()], None, []
    for level in range(depth):
        both = [
            solve(level, sub_dinv, sub_rhs, i, terms, True, f"solve_{level}_{i}")
            for i, terms in enumerate(parts)
        ]
        solved.append(jnp.concatenate([wide for wide, _ in both], axis=-1))
        held = spread([narrow for _, narrow in both], core, None if level else meta)
        *sums, carry = products(level, depth, meta, tiles, held, carry)
        parts = [(sums[n], *to_rows(sums[n + 1 : n + 4])) for n in range(0, len(sums), 4)]
    part = sum(term.astype(jnp.float32) for term in parts[0])
    other = lax.ppermute(part, "grp", [(0, 1), (1, 0)])
    (top,) = solve(None, anc_dinv, anc_rhs, 0, (part, other), False, "solve_top")
    return jnp.stack(solved)[None, :, None, None], top[None, None]


def solution(mesh):
    placed = (
        P("grp", None, "row", "col", None, None),
        P("grp", None, "row", "col", None, None),
        P("row", "col", None, None),
        P("row", "col", None, None),
        P("grp", "row", "col", None, None, None, None),
        P("grp", "row", "col", None, None),
        P("grp", "row", "col", None, None),
        P("grp", "row", "col", None),
    )
    return jax.shard_map(
        on_device,
        mesh=mesh,
        in_specs=placed,
        out_specs=(P("grp", None, "row", "col", None, None), P("row", "col", None, None)),
        check_vma=False,
    )
```

```python
import functools

import jax
import jax.numpy as jnp
import numpy as np
from jax import lax
from jax.experimental import pallas as pl
from jax.experimental.pallas import tpu as pltpu
from jax.sharding import PartitionSpec as P

Z, X = 8, 4
UNROLL = 4
EARLY = 6
PARTS = 2
VMEM_PRODUCTS = 8 * 1024 * 1024
PART = {0: (0, 0), 4: (0, 1), 6: (0, 2), 2: (0, 3), 1: (1, 0), 5: (1, 1), 7: (1, 2), 3: (1, 3)}
FIRST = {0: (0, 1), 3: (2, 6), 1: (3, 5), 2: (4, 7)}
BYZ = {0: 0, 7: 2, 1: 3, 6: 4, 2: 5, 5: 6, 3: 7}
BYX = {0: 0, 2: 1, 3: 2, 1: 3}


def places():
    table = np.zeros((2, 32), np.int32)
    for dx in range(X):
        for dz in range(Z):
            half, block = PART[dz]
            table[0, dx * Z + dz] = FIRST[dx][half] * 4 + block
            at = BYX[dx]
            if dz == 4:
                table[1, dx * Z + dz] = (8 + at // 2) * 4 + at % 2
            else:
                table[1, dx * Z + dz] = BYZ[dz] * 4 + at
    return table


def pairs(first, second):
    out = []
    for group, move in ((0, first), (1, second)):
        if move is None:
            continue
        for z in range(Z):
            for x in range(X):
                to = ((z + move[0]) % Z) * X + (x + move[1]) % X
                out.append((group * Z * X + z * X + x, group * Z * X + to))
    return out


def hop(array, first, second):
    return lax.ppermute(array, ("grp", "col"), pairs(first, second))


def spread(owns, core, tables_done):
    nears = []
    for own in owns:
        s1 = hop(own, (2, 0), (0, 1))
        s2 = hop(own, (-2, 0), (0, -1))
        s3 = hop(own, (4, 0), (0, 2))
        nears.append(jnp.stack([own, s3, s1, s2]))
    near = jnp.concatenate(nears, axis=-1)
    if tables_done is not None:
        near, _ = lax.optimization_barrier((near, tables_done))
    l1 = hop(near, (0, 1), (1, 0))
    l2 = hop(near, (0, -1), (-1, 0))
    far = hop(near, (-1, 0), None)
    l1, l2, far = lax.optimization_barrier((l1, l2, far))
    l3 = hop(l1, (0, 1), (1, 0))
    l4 = hop(jnp.where(core == 0, far, l2), (0, -1), (-1, 0))
    l3, l4 = lax.optimization_barrier((l3, l4))
    l5 = hop(jnp.where(core == 0, far, l3), (0, 1), (1, 0))
    l6 = hop(l4, (0, -1), (-1, 0))
    l7 = hop(l3[:2], None, (2, 0))
    l8 = hop(l4[2:], None, (-2, 0))
    return [near, far, l1, l2, l3, l4, l5, l6, l7, l8]


def pick(index, low, high, action):
    if high - low == 1:
        action(low)
        return
    middle = (low + high) // 2

    @pl.when(index < middle)
    def _():
        pick(index, low, middle, action)

    @pl.when(index >= middle)
    def _():
        pick(index, middle, high, action)


def product_kernel(level, first, held, dump, last, has_carry, meta, tiles, *refs):
    arrays, refs = refs[:held], refs[held:]
    if has_carry:
        carry, refs = refs[0], refs[1:]
    outs, (total, chosen, *rest) = refs[:-7], refs[-7:]
    number, factor, block, factor_sem, block_sem = rest
    load = pltpu.make_async_copy(tiles.at[0, 0, 0, level], factor, factor_sem)
    load.start()
    number[0] = 0

    def fetch(j, nothing):
        place = meta[level, 16 + j]
        index = lax.div(place, 4)

        @pl.when((index >= first) & (index < first + held))
        def _():
            n = number[0]
            chosen[n] = j
            number[0] = n + 1

            def begin(i):
                pltpu.make_async_copy(
                    arrays[i].at[lax.rem(place, 4)], block.at[n], block_sem.at[n]
                ).start()

            pick(index - first, 0, held, begin)

        return nothing

    lax.fori_loop(0, meta[level, 32], fetch, 0)
    if not last:
        for slot in range(dump):
            if has_carry:
                total[slot] = carry[4 + slot]
            else:
                total[slot] = jnp.zeros(total.shape[1:], jnp.float32)
    count = number[0]
    load.wait()

    def step(group, nothing):
        for k in range(UNROLL):
            n = group * UNROLL + k

            @pl.when(n < count)
            def _(n=n):
                pltpu.make_async_copy(arrays[0].at[0], block.at[n], block_sem.at[n]).wait()

        terms, targets = [], []
        for k in range(UNROLL):
            n = group * UNROLL + k
            live = n < count
            j = jnp.where(live, chosen[n], 0)
            targets.append(jnp.where(live, meta[level, j], dump))
            terms.append(jnp.dot(factor[j], block[n], preferred_element_type=jnp.float32))
        for target, term in zip(targets, terms):
            total[target] += term
        return nothing

    lax.fori_loop(0, lax.div(count + (UNROLL - 1), UNROLL), step, 0)
    if last:
        width = outs[0].shape[1]
        for n, out in enumerate(outs):
            cut = pl.ds((n // 4) * width, width)
            out[...] = total[n % 4, :, cut].astype(out.dtype)


def in_hbm(array):
    return pltpu.with_memory_space_constraint(array, pltpu.HBM)


def product_call(level, depth, meta, tiles, first, held, carry, last, name):
    rows, columns = held[0].shape[-2:]
    slots = tiles.shape[4]
    dump = 4 * (depth - level)
    vmem = pl.BlockSpec(memory_space=pltpu.VMEM)
    whole = jax.ShapeDtypeStruct((dump + 1, rows, columns), jnp.float32)
    outs, aliases = [whole], {}
    if last:
        parts = PARTS if dump > 4 else 1
        shape = (rows, columns // parts)
        sent = jax.ShapeDtypeStruct(shape, jnp.float32 if dump > 4 else jnp.bfloat16)
        outs = [jax.ShapeDtypeStruct(shape, jnp.float32), sent, sent, sent] * parts + [whole]
        aliases = {2 + len(held): len(outs) - 1}
    has_carry = carry is not None
    return pl.pallas_call(
        functools.partial(product_kernel, level, first, len(held), dump, last, has_carry),
        out_shape=outs,
        in_specs=[pl.BlockSpec(memory_space=pltpu.SMEM), pl.BlockSpec(memory_space=pltpu.HBM)]
        + [pl.BlockSpec(memory_space=pl.ANY)] * len(held)
        + [vmem] * has_carry,
        out_specs=[vmem] * len(outs),
        input_output_aliases=aliases,
        scratch_shapes=[
            pltpu.SMEM((slots,), jnp.int32),
            pltpu.SMEM((1,), jnp.int32),
            pltpu.VMEM((slots, rows, rows), jnp.bfloat16),
            pltpu.VMEM((slots, rows, columns), jnp.bfloat16),
            pltpu.SemaphoreType.DMA(()),
            pltpu.SemaphoreType.DMA((slots,)),
        ],
        compiler_params=pltpu.CompilerParams(vmem_limit_bytes=VMEM_PRODUCTS),
        cost_estimate=pl.CostEstimate(
            flops=slots * rows * rows * columns, bytes_accessed=4 * 1024 * 1024, transcendentals=0
        ),
        name=name,
    )(meta, in_hbm(tiles), *held, *([carry] if has_carry else []))


def products(level, depth, meta, tiles, held, carry):
    if EARLY:
        (carry,) = product_call(
            level, depth, meta, tiles, 0, held[:EARLY], carry, False, f"early_{level}"
        )
    return product_call(
        level, depth, meta, tiles, EARLY, held[EARLY:], carry, True, f"products_{level}"
    )


def solve_kernel(terms, narrow, inverse, rhs, *refs):
    rest = rhs[...].reshape(rhs.shape[-2:])
    if terms:
        amount = refs[0][...].astype(jnp.float32)
        for term in refs[1:terms]:
            amount = amount + term[...].astype(jnp.float32)
        rest = rest - amount
    solved = jnp.dot(
        inverse[...].reshape(inverse.shape[-2:]),
        rest,
        precision=lax.Precision.HIGHEST,
        preferred_element_type=jnp.float32,
    )
    refs[terms][...] = solved
    if narrow:
        refs[terms + 1][...] = solved.astype(jnp.bfloat16)


def solve(level, inverse, rhs, part, terms, narrow, name):
    rows, columns = terms[0].shape if terms else rhs.shape[-2:]
    vmem = pl.BlockSpec(memory_space=pltpu.VMEM)
    outs = [jax.ShapeDtypeStruct((rows, columns), jnp.float32)]
    if narrow:
        outs.append(jax.ShapeDtypeStruct((rows, columns), jnp.bfloat16))

    if level is None:
        operands = (inverse[0, 0], rhs[0, 0])
    elif level == 0:
        operands = (in_hbm(inverse), in_hbm(rhs))
    else:
        cut = slice(part * columns, (part + 1) * columns)
        operands = (inverse[0, level, 0, 0], rhs[0, level, 0, 0][:, cut])

    def of_level(array):
        if array.ndim == 2:
            return vmem
        block = (1,) * (array.ndim - 2) + array.shape[-2:]
        return pl.BlockSpec(block, lambda i: (0, level) + (0,) * (array.ndim - 2))

    return pl.pallas_call(
        functools.partial(solve_kernel, len(terms), narrow),
        out_shape=outs,
        grid=(1,),
        in_specs=[of_level(array) for array in operands] + [vmem] * len(terms),
        out_specs=[vmem] * len(outs),
        compiler_params=pltpu.CompilerParams(vmem_limit_bytes=6 * 1024 * 1024),
        cost_estimate=pl.CostEstimate(
            flops=12 * rows * rows * columns, bytes_accessed=2 * 1024 * 1024, transcendentals=0
        ),
        name=name,
    )(*operands, *terms)


def to_rows(sends):
    rows = 4
    return [
        lax.ppermute(sends[away - 1], "row", [(i, (i + away) % rows) for i in range(rows)])
        for away in (2, 1, 3)
    ]


def tables(tile_target, tile_source, tile_count):
    core, row, col = lax.axis_index("grp"), lax.axis_index("row"), lax.axis_index("col")
    levels = jnp.arange(tile_target.shape[0], dtype=jnp.int32)[:, None]
    level_of, row_of = tile_target // 4, tile_target % 4
    target = (level_of - levels) * 4 + (row_of - row) % 4
    dz = (tile_source // X - col // X) % Z
    dx = (tile_source % X - col % X) % X
    key = dx * Z + dz
    known = jnp.asarray(places())
    known = jnp.where(core == 0, known[0], known[1])
    match = key[:, :, None] == jnp.arange(Z * X, dtype=jnp.int32)
    place = jnp.sum(jnp.where(match, known, 0), axis=-1)
    live = jnp.arange(tile_target.shape[1], dtype=jnp.int32)[None] < tile_count[:, None]
    target = jnp.where(live, target, 0)
    counts = jnp.broadcast_to(tile_count[:, None], target.shape)
    return jnp.concatenate([target, place, counts], axis=1).astype(jnp.int32)


def on_device(sub_rhs, sub_dinv, anc_rhs, anc_dinv, tiles, tile_target, tile_source, tile_count):
    depth = sub_rhs.shape[1]
    core = lax.axis_index("grp")
    meta = tables(tile_target[0, 0, 0], tile_source[0, 0, 0], tile_count[0, 0, 0])
    parts, carry, solved = [()], None, []
    for level in range(depth):
        both = [
            solve(level, sub_dinv, sub_rhs, i, terms, True, f"solve_{level}_{i}")
            for i, terms in enumerate(parts)
        ]
        solved.append(jnp.concatenate([wide for wide, _ in both], axis=-1))
        held = spread([narrow for _, narrow in both], core, None if level else meta)
        *sums, carry = products(level, depth, meta, tiles, held, carry)
        parts = [(sums[n], *to_rows(sums[n + 1 : n + 4])) for n in range(0, len(sums), 4)]
    part = sum(term.astype(jnp.float32) for term in parts[0])
    other = lax.ppermute(part, "grp", [(0, 1), (1, 0)])
    (top,) = solve(None, anc_dinv, anc_rhs, 0, (part, other), False, "solve_top")
    return jnp.stack(solved)[None, :, None, None], top[None, None]


def solution(mesh):
    placed = (
        P("grp", None, "row", "col", None, None),
        P("grp", None, "row", "col", None, None),
        P("row", "col", None, None),
        P("row", "col", None, None),
        P("grp", "row", "col", None, None, None, None),
        P("grp", "row", "col", None, None),
        P("grp", "row", "col", None, None),
        P("grp", "row", "col", None),
    )
    return jax.shard_map(
        on_device,
        mesh=mesh,
        in_specs=placed,
        out_specs=(P("grp", None, "row", "col", None, None), P("row", "col", None, None)),
        check_vma=False,
    )
```
